32 devices in a mesh: row: 4 (over y, x), col: 8 (over z, core).
Axes of the slice: x: 2, y: 2, z: 4, core: 2. Of those that a mesh axis runs over, the one named last changes fastest.
Arguments:
- trailing_slab: bfloat16 [24576, 8192], P('row', 'col'), may hold values from -6 to 6
- panel_cols: bfloat16 [24576, 512], P('row', 'col'), may hold values from -0.25 to 0.25
- head_slab: bfloat16 [512, 8192], P('row', 'col'), may hold values from -6 to 6
- coupling: bfloat16 [2, 256, 256], replicated, may hold values from -0.25 to 0.25
- lower_inverses: bfloat16 [2, 256, 256], replicated, may hold values from -1.5 to 1.5, as said below
- upper_inverses: bfloat16 [2, 256, 256], replicated, may hold values from -1.5 to 1.5, as said below
Outputs:
- trailing: bfloat16 [24576, 8192], P('row', 'col')
The draws below stay inside these ranges and needn't reach their ends.
Inputs may be any that keep to these rules, and one draw needn't show every extreme that they name: `lower_inverses`: each of the two [256, 256] blocks is lower triangular with unit diagonal. `upper_inverses`: each of the two [256, 256] blocks is upper triangular with diagonal between 0.5 and 1.5.
All inputs are finite; a program needn't handle non-finite values.
Results may differ from the reference program's by a relative error of at most 0.0067.
Values may be sent and summed in bfloat16 or wider, within the bound.
No kernel may reach another device: no remote copies, remote signals or barrier semaphores. Data moves between devices by JAX's collectives and lax.ppermute only.
A program may use at most 128 MiB of HBM per device.

```python
import math
import jax
import jax.numpy as jnp
from jax import lax

NB = 256
TRAIL = 8192
ROWS_DEV = 6144
MROWS = 24576


def off_diagonal(key):
    values = jax.random.normal(key, (2, NB, NB), jnp.float32)
    return jnp.clip(values, -4.0, 4.0) * (0.5 / math.sqrt(NB))


def draw_lower_inverses(key, part):
    values = off_diagonal(jax.random.fold_in(key, 11))
    row_ids = lax.broadcasted_iota(jnp.int32, (2, NB, NB), 1)
    col_ids = lax.broadcasted_iota(jnp.int32, (2, NB, NB), 2)
    return (jnp.where(row_ids > col_ids, values, 0.0) + jnp.where(row_ids == col_ids, 1.0, 0.0)).astype(jnp.bfloat16)


def draw_upper_inverses(key, part):
    values = off_diagonal(jax.random.fold_in(key, 23))
    diag_values = jax.random.uniform(jax.random.fold_in(key, 37), (2, NB, NB), jnp.float32, 0.5, 1.5)
    row_ids = lax.broadcasted_iota(jnp.int32, (2, NB, NB), 1)
    col_ids = lax.broadcasted_iota(jnp.int32, (2, NB, NB), 2)
    return (jnp.where(row_ids < col_ids, values, 0.0) + jnp.where(row_ids == col_ids, diag_values, 0.0)).astype(jnp.bfloat16)


def block_scale(stream_key, shape, shards, least, top_value):
    factor_of = 1.0
    for axis_at, blocks in shards:
        heights = jax.random.uniform(jax.random.fold_in(jax.random.fold_in(stream_key, 6), axis_at), (blocks,), jnp.float32, least / len(shards), top_value / len(shards))
        factor_of = factor_of * jnp.repeat(jnp.exp(heights), shape[axis_at] // blocks).reshape((-1,) + (1,) * (len(shape) - 1 - axis_at))
    return factor_of


def scatter_about(stream_key, extent, scale, bound, pieces=(), dtype=jnp.bfloat16):
    level = block_scale(stream_key, extent, pieces, -0.22, 0.18) if pieces else 1.0
    drawn = jax.random.normal(stream_key, extent, jnp.float32) * scale * level
    return jnp.minimum(jnp.maximum(drawn, -bound), bound).astype(dtype)


def setup_inputs(seed: int = 0) -> dict:
    key_of = jax.random.split(jax.random.key(seed), 7)
    trailing_slab = scatter_about(key_of[0], (MROWS, TRAIL), 1.0, 6.0, ((0, 4), (1, 8)))
    panel_cols = scatter_about(key_of[1], (MROWS, 2 * NB), (2 * NB) ** -0.5, 0.25, ((0, 4), (1, 8)))
    head_slab = scatter_about(key_of[2], (2 * NB, TRAIL), 1.0, 6.0, ((0, 4), (1, 8)))
    coupling = scatter_about(key_of[3], (2, NB, NB), (2 * NB) ** -0.5, 0.25)
    lower_inverses = draw_lower_inverses(jax.random.fold_in(key_of[6], 71), 0)
    upper_inverses = draw_upper_inverses(jax.random.fold_in(key_of[6], 71), 0)
    return {"trailing_slab": trailing_slab, "panel_cols": panel_cols, "head_slab": head_slab, "coupling": coupling, "lower_inverses": lower_inverses, "upper_inverses": upper_inverses}


def product(left, right):
    return jnp.dot(left, right, preferred_element_type=jnp.float32)


def reference(trailing_slab, panel_cols, head_slab, coupling, lower_inverses, upper_inverses):
    lower_first = product(panel_cols[:, :NB], upper_inverses[0]).astype(jnp.bfloat16)
    upper_mid = product(lower_inverses[0], coupling[0]).astype(jnp.bfloat16)
    upper_first = product(lower_inverses[0], head_slab[:NB]).astype(jnp.bfloat16)
    lower_head = product(coupling[1], upper_inverses[0]).astype(jnp.bfloat16)
    panel_second = (panel_cols[:, NB:].astype(jnp.float32) - product(lower_first, upper_mid)).astype(jnp.bfloat16)
    lower_second = product(panel_second, upper_inverses[1]).astype(jnp.bfloat16)
    head_second = (head_slab[NB:].astype(jnp.float32) - product(lower_head, upper_first)).astype(jnp.bfloat16)
    upper_second = product(lower_inverses[1], head_second).astype(jnp.bfloat16)
    blocks = MROWS // ROWS_DEV
    slab_blocks = trailing_slab.reshape(blocks, ROWS_DEV, TRAIL)
    first_blocks = lower_first.reshape(blocks, ROWS_DEV, NB)
    second_blocks = lower_second.reshape(blocks, ROWS_DEV, NB)

    def update(items):
        slab_part, first_part, second_part = items
        result = slab_part.astype(jnp.float32) - product(first_part, upper_first) - product(second_part, upper_second)
        return result.astype(jnp.bfloat16)

    updated = lax.map(update, (slab_blocks, first_blocks, second_blocks))
    return updated.reshape(MROWS, TRAIL)
```

```python
import functools

import jax
import jax.numpy as jnp
from jax import lax
from jax.experimental import pallas as pl
from jax.experimental.pallas import tpu as pltpu
from jax.sharding import PartitionSpec as P


CORES = 2
F32 = jnp.float32
BF16 = jnp.bfloat16


def product(left, right):
    return jnp.dot(left, right, preferred_element_type=F32)


def product_wide(left, right):
    high = right.astype(BF16)
    low = (right - high.astype(F32)).astype(BF16)
    return product(left, high) + product(left, low)


def weights_kernel(parts, chips, ids_ref, *refs):
    row, col = ids_ref[0], ids_ref[1]
    chip, core = lax.div(col, CORES), lax.rem(col, CORES)
    head_refs = refs[:parts]
    coupling_ref, lower_ref, upper_ref, out_ref, head, both = refs[parts:]
    rows = head_refs[0].shape[0]
    width = coupling_ref.shape[1]
    for at in range(parts):
        start = pl.multiple_of((row ^ at) * rows, rows)
        head[pl.ds(start, rows), :] = head_refs[at][...]
    upper_mid = product(lower_ref[0], coupling_ref[0]).astype(BF16)
    lower_head = product(coupling_ref[1], upper_ref[0]).astype(BF16)
    upper_first = product(lower_ref[0], head[:width, :]).astype(BF16)
    head_second = (head[width:, :].astype(F32) - product(lower_head, upper_first)).astype(BF16)
    upper_second = product(lower_ref[1], head_second).astype(BF16)
    second = product(upper_ref[1], upper_second)
    rest = upper_first.astype(F32) - product_wide(upper_mid, second)
    both[:width, :] = product_wide(upper_ref[0], rest).astype(BF16)
    both[width:, :] = second.astype(BF16)
    depth = out_ref.shape[0] // (chips * CORES)
    for at in range(chips * CORES):
        source = lax.rem(chip + chips - at // CORES, chips) * CORES + (core ^ (at % CORES))
        start = pl.multiple_of(source * depth, depth)
        out_ref[at * depth : (at + 1) * depth, :] = both[pl.ds(start, depth), :]


def weights(ids, heads, coupling, lower_inverses, upper_inverses, chips):
    depth = 2 * coupling.shape[1]
    columns = heads[0].shape[1]
    vmem = pl.BlockSpec(memory_space=pltpu.VMEM)
    return pl.pallas_call(
        functools.partial(weights_kernel, len(heads), chips),
        out_shape=jax.ShapeDtypeStruct((depth, columns), BF16),
        in_specs=[pl.BlockSpec(memory_space=pltpu.SMEM)] + [vmem] * (len(heads) + 3),
        out_specs=vmem,
        scratch_shapes=[pltpu.VMEM((depth, columns), BF16), pltpu.VMEM((depth, columns), BF16)],
        compiler_params=pltpu.CompilerParams(vmem_limit_bytes=16 << 20),
        cost_estimate=pl.CostEstimate(flops=2 * 10 * 256 * 256 * columns, bytes_accessed=8 * columns * 256, transcendentals=0),
        name="weights",
    )(ids, *heads, coupling, lower_inverses, upper_inverses)


def update_kernel(pieces, slab_ref, weights_ref, *refs):
    out_ref = refs[-1]
    left = jnp.concatenate([ref[...] for ref in refs[:pieces]], axis=0)
    change = lax.dot_general(left, weights_ref[...], (((0,), (0,)), ((), ())), preferred_element_type=F32)
    out_ref[...] = (slab_ref[...].astype(F32) - change).astype(BF16)


def update(slab, weights_all, pieces, start, rows, result):
    columns = slab.shape[1]
    tile = min(512, rows)
    first = start // tile
    in_specs = [
        pl.BlockSpec((tile, columns), lambda i: (first + i, 0)),
        pl.BlockSpec(weights_all.shape, lambda i: (0, 0), pipeline_mode=pl.Buffered(1)),
    ]
    for array, offset in pieces:
        at = (start - offset) // tile
        in_specs.append(pl.BlockSpec((array.shape[0], tile), functools.partial(lambda at, i: (0, at + i), at)))
    operands = [slab, weights_all] + [array for array, _ in pieces]
    aliases = {}
    if result is not None:
        in_specs.append(pl.BlockSpec(memory_space=pl.ANY))
        aliases = {len(operands): 0}
        operands.append(result)
    return pl.pallas_call(
        functools.partial(update_kernel, len(pieces)),
        grid=(rows // tile,),
        out_shape=jax.ShapeDtypeStruct(slab.shape, slab.dtype),
        in_specs=in_specs,
        out_specs=pl.BlockSpec((tile, columns), lambda i: (first + i, 0)),
        input_output_aliases=aliases,
        compiler_params=pltpu.CompilerParams(dimension_semantics=("arbitrary",), vmem_limit_bytes=16 << 20),
        cost_estimate=pl.CostEstimate(
            flops=2 * rows * columns * weights_all.shape[0],
            bytes_accessed=2 * rows * columns * 2,
            transcendentals=0,
        ),
        name="update",
    )(*operands)


def later(value, done):
    return lax.optimization_barrier((value, done))[0]


def on_device(rows_of, cols_of, groups, trailing_slab, panel_cols, head_slab, coupling, lower_inverses, upper_inverses):
    chips = cols_of // CORES
    ring = [(c, (c + CORES) % cols_of) for c in range(cols_of)]
    sibling = [(c, c ^ 1) for c in range(cols_of)]
    panel = panel_cols.T

    def send(value, pairs, axis="col"):
        return lax.ppermute(value, axis, pairs)

    arrived = []
    panel_sibling = None
    behind = None
    for g, group in enumerate(groups):
        source = panel if behind is None else later(panel, behind)
        held = [source[:, start : start + size] for start, size in group]
        for step in range(1, chips):
            for i in range(len(group)):
                held[i] = send(held[i], ring)
                if panel_sibling is None:
                    first = held[i]
                    panel_sibling = send(later(panel, first), sibling)
                arrived.append((g, i, held[i], send(held[i], sibling)))
            if step == chips - 2:
                behind = held[-1]

    head_slab = later(head_slab, first)
    heads = [head_slab]
    for shift in range(1, rows_of):
        heads.append(send(head_slab, [(r, r ^ shift) for r in range(rows_of)], "row"))
    ids = jnp.stack([lax.axis_index("row"), lax.axis_index("col")]).astype(jnp.int32)
    weights_all = weights(ids, heads, coupling, lower_inverses, upper_inverses, chips)

    result = None
    for g, group in enumerate(groups):
        for i, (start, size) in enumerate(group):
            pieces = [(panel, 0), (panel_sibling, 0)]
            for at, chunk, own, other in arrived:
                if (at, chunk) == (g, i):
                    pieces += [(own, start), (other, start)]
            result = update(trailing_slab, weights_all, pieces, start, size, result)
    return result


def plan(rows):
    unit = rows // 6
    sizes = [[unit, unit, unit], [unit, unit, unit]]
    groups, start = [], 0
    for group in sizes:
        groups.append([])
        for size in group:
            groups[-1].append((start, size))
            start += size
    return groups


def solution(mesh):
    in_specs = (P("row", "col"), P("row", "col"), P("row", "col"), P(), P(), P())
    out_specs = P("row", "col")
    rows_of, cols_of = mesh.shape["row"], mesh.shape["col"]

    def body(*arrays):
        groups = plan(arrays[0].shape[0])
        return on_device(rows_of, cols_of, groups, *arrays)

    return jax.shard_map(body, mesh=mesh, in_specs=in_specs, out_specs=out_specs, check_vma=False)
```
